32 devices in a mesh: stn: 8 (over y, x, core), seg: 4 (over z).
Axes of the slice: x: 2, y: 2, z: 4, core: 2. Of those that a mesh axis runs over, the one named last changes fastest.
Arguments:
- spectra: bfloat16 [512, 5, 4, 2, 2048], P('stn', None, 'seg'), may hold values from -6 to 6
- segment_valid: int32 [512, 4], P('stn', 'seg'), may hold values 0 or 1
- pair_live: int32 [8, 5], P('stn'), may hold values 0 or 1
Outputs:
- cross: float32 [512, 5, 5, 2, 128], P(('stn', 'seg'))
The draws below stay inside these ranges and needn't reach their ends.
All inputs are finite; a program needn't handle non-finite values. No bound on the sum of `segment_valid` or of `pair_live` on one device may be relied on, other than what follows from the above.
Results may differ from the reference program's by a relative error of at most 0.0003.
Values may be sent and summed in bfloat16 or wider, within the bound.
No kernel may reach another device: no remote copies, remote signals or barrier semaphores. Data moves between devices by JAX's collectives and lax.ppermute only.
A program may use at most 64 MiB of HBM per device.

```python
import math
import jax
import jax.numpy as jnp
from jax import lax

STN_BLK = 64
CH = 5
FREQ = 2048
PAIRS = 5
STATIONS = 512
SEGMENTS = 4
NBLK = 8


def set_ends(entries, key, low, largest):
    longest = entries.shape.index(max(entries.shape))
    spots = []
    for shift in (0, 1):
        where = [jax.random.randint(jax.random.fold_in(key, axis), (), 0, length) for axis, length in enumerate(entries.shape)]
        where[longest] = (where[longest] + shift) % entries.shape[longest]
        spots.append(tuple(where))
    return entries.at[spots[0]].set(low).at[spots[1]].set(largest)


def shard_levels(rng, shape, split, smallest, largest):
    def one(dim, parts):
        heights = jax.random.uniform(jax.random.fold_in(jax.random.fold_in(rng, 6), dim), (parts,), jnp.float32, smallest / len(split), largest / len(split))
        return jnp.repeat(jnp.exp(heights), shape[dim] // parts).reshape((-1,) + (1,) * (len(shape) - dim - 1))

    factor_of = one(*split[0])
    for cut in split[1:]:
        factor_of = factor_of * one(*cut)
    return factor_of


def normal_values(key, dims, deviation, limit, cuts=(), held_as=jnp.bfloat16):
    values = jax.random.normal(key, dims, jnp.float32) * deviation
    if len(cuts) > 0:
        values = shard_levels(key, dims, cuts, -0.22, 0.18) * values
    return jnp.clip(values, min=-limit, max=limit).astype(held_as)


def setup_inputs(seed: int = 0) -> dict:
    keys = jax.random.split(jax.random.key(seed), 4)
    spectra = normal_values(keys[0], (STATIONS, CH, SEGMENTS, 2, FREQ), 1.0, 6.0, ((0, 8), (2, 4)))
    segment_valid = set_ends((jax.random.randint(keys[1], (STATIONS, SEGMENTS), 0, 4) < 3).astype(jnp.int32), jax.random.fold_in(keys[1], 1), 0, 1)
    pair_live = set_ends((jax.random.randint(keys[2], (NBLK, PAIRS), 0, 4) < 3).astype(jnp.int32), jax.random.fold_in(keys[2], 1), 0, 1)
    return dict(spectra=spectra, segment_valid=segment_valid, pair_live=pair_live)


def reference(spectra, segment_valid, pair_live):
    masked = spectra * segment_valid.astype(jnp.bfloat16)[:, None, :, None, None]
    block_count = STATIONS // STN_BLK
    blocks = masked.reshape(block_count, STN_BLK, CH, SEGMENTS, 2, FREQ)
    ref_rows = blocks[:, :, 2:4]
    factor = 1.0 / math.sqrt(SEGMENTS * FREQ)

    def one_block(block_id):
        local_rows = blocks[block_id].astype(jnp.float32)
        pieces = []
        for offset in range(PAIRS):
            remote = ref_rows[(block_id - offset) % block_count].astype(jnp.float32)
            real_part = jnp.einsum('icsaf,jhsaf->icjh', local_rows, remote, precision=lax.Precision.HIGHEST)
            imag_part = jnp.einsum('icsf,jhsf->icjh', local_rows[:, :, :, 1], remote[:, :, :, 0], precision=lax.Precision.HIGHEST)
            imag_part = imag_part - jnp.einsum('icsf,jhsf->icjh', local_rows[:, :, :, 0], remote[:, :, :, 1], precision=lax.Precision.HIGHEST)
            pair_term = jnp.stack([real_part, imag_part], axis=2).reshape(STN_BLK, CH, 2, STN_BLK * 2)
            pieces.append(pair_term * factor * pair_live[block_id, offset].astype(jnp.float32))
        return jnp.stack(pieces, axis=2)
    result = lax.map(one_block, jnp.arange(block_count, dtype=jnp.int32))
    return result.reshape(STATIONS, CH, PAIRS, 2, STN_BLK * 2)
```

```python
import functools
import math

import jax
import jax.numpy as jnp
from jax import lax
from jax.experimental import pallas as pl
from jax.experimental.pallas import tpu as pltpu
from jax.sharding import PartitionSpec as P

PAIRS = 5
CHUNKS = 4
LANES = 128
VMEM = pl.BlockSpec(memory_space=pltpu.VMEM)
HBM = pl.BlockSpec(memory_space=pl.ANY)
SMEM = pl.BlockSpec(memory_space=pltpu.SMEM)
F32 = jnp.float32
BF16 = jnp.bfloat16


def params(mib):
    return pltpu.CompilerParams(vmem_limit_bytes=mib * 2**20)


def iota(shape, dim):
    return lax.broadcasted_iota(jnp.int32, shape, dim)


def dot_t(a, b):
    return lax.dot_general(a, b, (((1,), (1,)), ((), ())), preferred_element_type=F32)


def extract_kernel(x_hbm, valid_ref, full_ref, *rest):
    *chunk_refs, buf, sem = rest
    copy = pltpu.make_async_copy(x_hbm.at[:, 2:4], buf, sem)
    copy.start()
    block = buf.shape[0]
    rows = 4 * block
    half = rows // 2
    spread = (iota((block, rows), 1) // 4 == iota((block, rows), 0)).astype(BF16)
    valid = jnp.broadcast_to(valid_ref[...], (8, block)).astype(F32).astype(BF16)
    valid = jnp.dot(valid, spread, preferred_element_type=F32)[:1]
    to, frm = iota((rows, rows), 0), iota((rows, rows), 1)
    source = jnp.where(to < half, 2 * to, 2 * (to - half) + 1)
    pick = jnp.where(frm == source, jnp.broadcast_to(valid, (rows, rows)), 0.0).astype(BF16)
    copy.wait()
    full = jnp.dot(pick, buf[...].reshape(rows, buf.shape[-1]), preferred_element_type=F32).astype(BF16)
    full_ref[...] = full
    width = half // len(chunk_refs)
    for k, chunk_ref in enumerate(chunk_refs):
        for part in range(2):
            at = part * half + k * width
            chunk_ref[part * width : (part + 1) * width] = full[at : at + width]


def store_tiles(g_ref, value):
    for tile in range(g_ref.shape[0]):
        g_ref[tile] = value[:, tile * LANES : (tile + 1) * LANES]


def combine(g_ref, out_keep, out_send, seg, members):
    tiles, rows = g_ref.shape[0], g_ref.shape[1] // members
    sign = jnp.where(iota((1, LANES), 1) < LANES // 2, 1.0, -1.0)
    for slot in range(members):
        at = pl.multiple_of((seg ^ slot) * rows, 8)
        out = out_send if slot % 2 else out_keep
        even = [g_ref[t, pl.ds(at, rows // 2, stride=2), :] for t in range(tiles)]
        odd = [g_ref[t, pl.ds(at + 1, rows // 2, stride=2), :] for t in range(tiles)]
        if tiles == 1:
            out[slot // 2] = pltpu.roll(odd[0], LANES // 2, 1) + sign * even[0]
        for t in range(tiles // 2):
            u = t + tiles // 2
            out[slot // 2, :, t * LANES : (t + 1) * LANES] = even[t] + odd[u]
            out[slot // 2, :, u * LANES : (u + 1) * LANES] = odd[t] - even[u]


def own_kernel(members, x_ref, valid_ref, full_ref, a_ref, keep_ref, send_ref, g_ref):
    block = x_ref.shape[0]
    rows = a_ref.shape[0]
    pick = (iota((rows, block), 0) // (rows // block) == iota((rows, block), 1)).astype(BF16)
    valid = jnp.broadcast_to(valid_ref[...], (8, block)).astype(F32).astype(BF16)
    valid = dot_t(pick, valid)[:, :1].astype(BF16)
    a_ref[...] = x_ref[...].reshape(a_ref.shape) * valid
    store_tiles(g_ref, dot_t(a_ref[...], full_ref[...]))
    combine(g_ref, keep_ref, send_ref, lax.axis_index("seg"), members)


def chunk_kernel(members, a_ref, sib_ref, own_ref, four_ref, low_ref, high_ref, keep_ref, send_ref, b_ref, g_ref):
    seg, stn = lax.axis_index("seg"), lax.axis_index("stn")
    first, odd = stn % 2 == 0, (stn // 2) % 2 == 1
    width = own_ref.shape[0] // 2

    def fill(which, column, ref):
        for part in range(2):
            at = (2 * part + column) * width
            b_ref[which, at : at + width] = ref[part * width : (part + 1) * width]

    def both(two_ref):
        fill(0, 0, two_ref)
        fill(0, 1, four_ref)

        @pl.when(first)
        def _():
            fill(1, 0, own_ref)
            fill(1, 1, two_ref)

        @pl.when(jnp.logical_not(first))
        def _():
            fill(1, 0, two_ref)
            fill(1, 1, four_ref)

    pl.when(odd)(lambda: both(low_ref))
    pl.when(jnp.logical_not(odd))(lambda: both(high_ref))
    store_tiles(g_ref.at[0], dot_t(a_ref[...], b_ref[0]))
    store_tiles(g_ref.at[1], dot_t(sib_ref[...], b_ref[1]))
    for which in range(2):
        combine(g_ref.at[which], keep_ref.at[which], send_ref.at[which], seg, members)


def add_kernel(keep_ref, got_ref, new_keep_ref, new_send_ref):
    for slot in range(keep_ref.shape[0]):
        out = new_send_ref if slot % 2 else new_keep_ref
        out[slot // 2] = keep_ref[slot] + got_ref[slot]


def add_last_kernel(keep_ref, got_ref, *out_refs):
    for which in range(2):
        for slot in range(2):
            out_refs[2 * which + slot][...] = keep_ref[which, slot] + got_ref[which, slot]


def final_kernel(factor, chunks, live_ref, *refs):
    *in_refs, out_ref = refs
    pairs = [in_refs[i][...] + in_refs[i + 1][...] for i in range(0, len(in_refs), 2)]
    own, mine, theirs = pairs[0], pairs[1 : 1 + chunks], pairs[1 + chunks :]
    rows = out_ref.shape[0] // (2 * PAIRS)
    lanes = out_ref.shape[1]
    for offset in range(PAIRS):
        scale = live_ref[0, offset].astype(F32) * factor
        for part in range(2):
            if offset == 0:
                value = own[:, part * lanes : (part + 1) * lanes]
            else:
                width = lanes // chunks
                at = (2 * part + (offset - 1) // 2) * width
                value = jnp.concatenate([t[:, at : at + width] for t in (theirs if offset % 2 else mine)], axis=1)
            out_ref[pl.ds(2 * offset + part, rows, stride=2 * PAIRS), :] = value * scale


def per_device(spectra, segment_valid, pair_live):
    block, channels, seg_local, _, freq = spectra.shape
    blocks, members = lax.axis_size("stn"), lax.axis_size("seg")
    factor = 1.0 / math.sqrt(seg_local * members * freq)
    valid = segment_valid.reshape(1, block)
    rows, per = 2 * block * channels, block * channels // members
    width = 2 * block // CHUNKS

    full, *own = pl.pallas_call(
        extract_kernel,
        in_specs=[HBM, VMEM],
        out_specs=[VMEM] * (1 + CHUNKS),
        out_shape=[jax.ShapeDtypeStruct((4 * block, freq), BF16)]
        + [jax.ShapeDtypeStruct((2 * width, freq), BF16)] * CHUNKS,
        scratch_shapes=[pltpu.VMEM((block, 2, 1, 2, freq), BF16), pltpu.SemaphoreType.DMA],
        compiler_params=params(12),
    )(spectra, valid)

    ids = range(blocks)
    four = [lax.ppermute(c, "stn", [((i - 4) % blocks, i) for i in ids]) for c in own]
    low = [lax.ppermute(c, "stn", [((i - 2) % blocks, i) for i in ids if i // 2 % 2 == 1]) for c in own]
    high = [lax.ppermute(c, "stn", [((i + 2) % blocks, i) for i in ids if i // 2 % 2 == 0]) for c in four]

    half = members // 2
    a, keep, send = pl.pallas_call(
        functools.partial(own_kernel, members),
        in_specs=[VMEM] * 3,
        out_specs=[VMEM] * 3,
        out_shape=[jax.ShapeDtypeStruct((rows, freq), BF16)]
        + [jax.ShapeDtypeStruct((half, per, 4 * block), F32)] * 2,
        scratch_shapes=[pltpu.VMEM((4 * block // LANES, rows, LANES), F32)],
        compiler_params=params(16),
    )(spectra, valid, full)
    sibling = lax.ppermute(a, "stn", [(i ^ 1, i) for i in ids])

    def to(distance):
        return [(i ^ distance, i) for i in range(members)]

    def halve(keep, send, distance, lead):
        got = lax.ppermute(send, "seg", to(distance))
        shape = (*lead, keep.shape[len(lead)] // 2, *keep.shape[len(lead) + 1 :])
        if lead:
            shape = (shape[0] * shape[1], *shape[2:])
        flat = lambda v: v.reshape((-1, *v.shape[-2:]))
        new = pl.pallas_call(
            add_kernel,
            in_specs=[VMEM] * 2,
            out_specs=[VMEM] * 2,
            out_shape=[jax.ShapeDtypeStruct(shape, F32)] * 2,
            compiler_params=params(8),
        )(flat(keep), flat(got))
        return [v.reshape((*lead, -1, *v.shape[-2:])) for v in new]

    distance = 1
    while 2 * distance < members:
        keep, send = halve(keep, send, distance, ())
        distance *= 2
    final = [keep.reshape(keep.shape[-2:]), lax.ppermute(send, "seg", to(distance)).reshape(keep.shape[-2:])]

    mine, theirs = [], []
    for k in range(CHUNKS):
        keep, send = pl.pallas_call(
            functools.partial(chunk_kernel, members),
            in_specs=[VMEM] * 6,
            out_specs=[VMEM] * 2,
            out_shape=[jax.ShapeDtypeStruct((2, half, per, 4 * width), F32)] * 2,
            scratch_shapes=[pltpu.VMEM((2, 4 * width, freq), BF16), pltpu.VMEM((2, 4 * width // LANES, rows, LANES), F32)],
            compiler_params=params(16),
        )(a, sibling, own[k], four[k], low[k], high[k])
        distance = 1
        while 4 * distance < members:
            keep, send = halve(keep, send, distance, (2,))
            distance *= 2
        got = lax.ppermute(send, "seg", to(distance))
        keep_own, send_own, keep_sib, send_sib = pl.pallas_call(
            add_last_kernel,
            in_specs=[VMEM] * 2,
            out_specs=[VMEM] * 4,
            out_shape=[jax.ShapeDtypeStruct((per, 4 * width), F32)] * 4,
            compiler_params=params(8),
        )(keep, got)
        distance *= 2
        got_own = lax.ppermute(send_own, "seg", to(distance))
        cross = [
            (i * members + j, (i ^ 1) * members + (j ^ distance)) for i in ids for j in range(members)
        ]
        got_sib = lax.ppermute(send_sib, ("stn", "seg"), cross)
        kept_sib = lax.ppermute(keep_sib, "stn", [(i ^ 1, i) for i in ids])
        mine += [keep_own, got_own]
        theirs += [kept_sib, got_sib]

    out = pl.pallas_call(
        functools.partial(final_kernel, factor, CHUNKS),
        in_specs=[SMEM] + [VMEM] * (2 + 4 * CHUNKS),
        out_specs=VMEM,
        out_shape=jax.ShapeDtypeStruct((2 * PAIRS * per, 2 * block), F32),
        compiler_params=params(12),
    )(pair_live, *final, *mine, *theirs)
    return out.reshape(block // members, channels, PAIRS, 2, 2 * block)


def solution(mesh):
    return jax.shard_map(
        per_device,
        mesh=mesh,
        in_specs=(P("stn", None, "seg", None, None), P("stn", "seg"), P("stn", None)),
        out_specs=P(("stn", "seg"), None, None, None, None),
        check_vma=False,
    )
```

```python
import functools
import math

import jax
import jax.numpy as jnp
from jax import lax
from jax.experimental import pallas as pl
from jax.experimental.pallas import tpu as pltpu
from jax.sharding import PartitionSpec as P

PAIRS = 5
CHUNKS = 4
UNITS = 2
STEPS = True
COST = None
LANES = 128
VMEM = pl.BlockSpec(memory_space=pltpu.VMEM)
HBM = pl.BlockSpec(memory_space=pltpu.HBM)
SMEM = pl.BlockSpec(memory_space=pltpu.SMEM)
F32 = jnp.float32
BF16 = jnp.bfloat16


def params(mib):
    return pltpu.CompilerParams(vmem_limit_bytes=mib * 2**20)


def iota(shape, dim):
    return lax.broadcasted_iota(jnp.int32, shape, dim)


def dot_t(a, b):
    return lax.dot_general(a, b, (((1,), (1,)), ((), ())), preferred_element_type=F32)


def extract_kernel(x_hbm, valid_hbm, full_ref, row_ref, *rest):
    *chunk_refs, buf, valid_buf, sems = rest
    copy = pltpu.make_async_copy(x_hbm.at[:, 2:4], buf, sems.at[0])
    copy.start()
    small = pltpu.make_async_copy(valid_hbm, valid_buf, sems.at[1])
    small.start()
    block = buf.shape[0]
    rows = 4 * block
    half = rows // 2
    spread = (iota((block, rows), 1) // 4 == iota((block, rows), 0)).astype(BF16)
    to, frm = iota((rows, rows), 0), iota((rows, rows), 1)
    source = jnp.where(to < half, 2 * to, 2 * (to - half) + 1)
    small.wait()
    valid = jnp.broadcast_to(valid_buf[...], row_ref.shape).astype(F32).astype(BF16)
    row_ref[...] = valid
    valid = jnp.dot(valid, spread, preferred_element_type=F32)[:1]
    pick = jnp.where(frm == source, jnp.broadcast_to(valid, (rows, rows)), 0.0).astype(BF16)
    copy.wait()
    full = jnp.dot(pick, buf[...].reshape(rows, buf.shape[-1]), preferred_element_type=F32).astype(BF16)
    full_ref[...] = full
    width = half // CHUNKS
    for k, chunk_ref in enumerate(chunk_refs):
        for part in range(2):
            at = part * half + k * width
            chunk_ref[part * width : (part + 1) * width] = full[at : at + width]


def store_tiles(g_ref, value):
    for tile in range(g_ref.shape[0]):
        g_ref[tile] = value[:, tile * LANES : (tile + 1) * LANES]


def combine(g_ref, out_keep, out_send, seg, members):
    tiles, rows = g_ref.shape[0], g_ref.shape[1] // members
    sign = jnp.where(iota((1, LANES), 1) < LANES // 2, 1.0, -1.0)
    for slot in range(members):
        at = pl.multiple_of((seg ^ slot) * rows, 8)
        out = out_send if slot % 2 else out_keep
        even = [g_ref[t, pl.ds(at, rows // 2, stride=2), :] for t in range(tiles)]
        odd = [g_ref[t, pl.ds(at + 1, rows // 2, stride=2), :] for t in range(tiles)]
        if tiles == 1:
            out[slot // 2] = pltpu.roll(odd[0], LANES // 2, 1) + sign * even[0]
        for t in range(tiles // 2):
            u = t + tiles // 2
            out[slot // 2, :, t * LANES : (t + 1) * LANES] = even[t] + odd[u]
            out[slot // 2, :, u * LANES : (u + 1) * LANES] = odd[t] - even[u]


def own_kernel(members, x_ref, valid_ref, full_ref, a_ref, keep_ref, send_ref, g_ref):
    block = x_ref.shape[0]
    rows = a_ref.shape[0]
    pick = (iota((rows, block), 0) // (rows // block) == iota((rows, block), 1)).astype(BF16)
    valid = dot_t(pick, valid_ref[...])[:, :1].astype(BF16)
    a_ref[...] = x_ref[...].reshape(a_ref.shape) * valid
    store_tiles(g_ref, dot_t(a_ref[...], full_ref[...]))
    combine(g_ref, keep_ref, send_ref, lax.axis_index("seg"), members)


def place(index):
    return (lax.axis_index("stn") >> index) & 1 == 1


def choose_kernel(own_ref, four_ref, out_ref):
    odd = place(1)

    @pl.when(odd)
    def _():
        out_ref[...] = four_ref[...]

    @pl.when(jnp.logical_not(odd))
    def _():
        out_ref[...] = own_ref[...]


def pair_kernel(members, at, early, a_ref, sib_ref, *refs):
    *piece_refs, full_ref, keep_ref, send_ref, b_ref, g_ref = refs
    seg = lax.axis_index("seg")
    width = piece_refs[0].shape[0] // 2
    half = b_ref.shape[1] // 2
    for i, piece_ref in enumerate(piece_refs):
        for part in range(2):
            to = part * half + i * width
            b_ref[0, to : to + width] = piece_ref[part * width : (part + 1) * width]
    if early:
        second = place(0)

        @pl.when(second)
        def _():
            b_ref[1] = b_ref[0]

        @pl.when(jnp.logical_not(second))
        def _():
            for part in range(2):
                frm = part * (full_ref.shape[0] // 2) + at
                b_ref[1, part * half : (part + 1) * half] = full_ref[frm : frm + half]

    store_tiles(g_ref.at[0], dot_t(a_ref[...], b_ref[0]))
    store_tiles(g_ref.at[1], dot_t(sib_ref[...], b_ref[1 if early else 0]))
    for which in range(2):
        combine(g_ref.at[which], keep_ref.at[which], send_ref.at[which], seg, members)


def add_kernel(keep_ref, got_ref, new_keep_ref, new_send_ref):
    for slot in range(keep_ref.shape[0]):
        out = new_send_ref if slot % 2 else new_keep_ref
        out[slot // 2] = keep_ref[slot] + got_ref[slot]


def home_kernel(*refs):
    *in_refs, out_ref = refs
    for k in range(out_ref.shape[0]):
        out_ref[k] = in_refs[2 * k][1] + in_refs[2 * k + 1][1]


def final_kernel(factor, live_ref, *refs):
    own_keep_ref, own_got_ref, *in_refs, early_ref, late_ref, out_ref = refs
    own = own_keep_ref[...] + own_got_ref[...]
    mine = [in_refs[i][0] + in_refs[i + 1][0] for i in range(0, len(in_refs), 2)]
    theirs = [r[i] for r in (early_ref, late_ref) for i in range(r.shape[0])]
    second = jnp.broadcast_to(lax.axis_index("stn") & 1, mine[0].shape) == 1
    by_offset = {
        4: mine[0::2],
        2: mine[1::2],
        1: [jnp.where(second, e, l) for e, l in zip(theirs[0::2], theirs[1::2])],
        3: [jnp.where(second, l, e) for e, l in zip(theirs[0::2], theirs[1::2])],
    }
    rows = out_ref.shape[0] // (2 * PAIRS)
    width = LANES // UNITS
    for offset in range(PAIRS):
        scale = live_ref[0, offset].astype(F32) * factor
        for part in range(2):
            if offset == 0:
                value = own[:, part * LANES : (part + 1) * LANES]
            else:
                value = jnp.concatenate([t[:, part * width : (part + 1) * width] for t in by_offset[offset]], axis=1)
            out_ref[pl.ds(2 * offset + part, rows, stride=2 * PAIRS), :] = value * scale


def tie(values, *others):
    return lax.optimization_barrier((values, others))[0]


def per_device(spectra, segment_valid, pair_live):
    block, channels, seg_local, _, freq = spectra.shape
    blocks, members = lax.axis_size("stn"), lax.axis_size("seg")
    factor = 1.0 / math.sqrt(seg_local * members * freq)
    rows, per, half = 2 * block * channels, block * channels // members, members // 2
    width = 2 * block // CHUNKS
    ids = range(blocks)

    def call(kernel, outs, operands, mib, scratch=(), specs=None, cost=COST):
        return pl.pallas_call(
            kernel,
            in_specs=specs or [VMEM] * len(operands),
            out_specs=[VMEM] * len(outs),
            out_shape=[jax.ShapeDtypeStruct(*out) for out in outs],
            scratch_shapes=list(scratch),
            compiler_params=params(mib),
            cost_estimate=cost and pl.CostEstimate(flops=cost, bytes_accessed=cost, transcendentals=0),
        )(*operands)

    full, valid, *own = call(
        extract_kernel,
        [((4 * block, freq), BF16), ((8, block), BF16)] + [((2 * width, freq), BF16)] * CHUNKS,
        [pltpu.with_memory_space_constraint(v, pltpu.HBM) for v in (spectra, segment_valid.reshape(1, block))],
        12,
        [
            pltpu.VMEM((block, 2, 1, 2, freq), BF16),
            pltpu.VMEM((1, block), jnp.int32),
            pltpu.SemaphoreType.DMA((2,)),
        ],
        [HBM] * 2,
    )

    def exchange(c, distance):
        return lax.ppermute(c, "stn", [(i ^ distance, i) for i in ids])

    def halve(keep, send, distance, kinds):
        got = lax.ppermute(send, "seg", [(i ^ distance, i) for i in range(members)])
        lead = (kinds,) if kinds else ()
        slots = keep.shape[len(lead)]
        if slots == 1:
            return keep.reshape(*lead, *keep.shape[-2:]), got.reshape(*lead, *keep.shape[-2:])
        shape = (max(kinds, 1) * slots // 2, *keep.shape[-2:])
        new = call(add_kernel, [(shape, F32)] * 2, [v.reshape(-1, *shape[1:]) for v in (keep, got)], 8)
        return [v.reshape(*lead, slots // 2, *shape[1:]) for v in new]

    def reduce(keep, send, kinds):
        steps = []
        distance = 1
        while distance < members:
            keep, send = halve(keep, send, distance, kinds)
            steps.append(keep if 2 * distance < members else send)
            distance *= 2
        return (keep, send), steps

    four = [lax.ppermute(c, "stn", [((i - 4) % blocks, i) for i in ids]) for c in own]
    two = []
    for k in range(CHUNKS):
        (c,) = call(choose_kernel, [((2 * width, freq), BF16)], [own[k], four[k]], 8)
        two.append(exchange(c, 2))

    a, keep, send = call(
        functools.partial(own_kernel, members),
        [((rows, freq), BF16)] + [((half, per, 4 * block), F32)] * 2,
        [spectra, valid, full],
        16,
        [pltpu.VMEM((4 * block // LANES, rows, LANES), F32)],
    )
    sibling = exchange(a, 1)
    (own_keep, own_got), own_steps = reduce(keep, send, 0)

    pieces, steps = [], [own_steps]
    size = 4 * block // UNITS
    for unit in range(2 * UNITS):
        early, which = unit % 2 == 0, unit // 2
        some = (four if early else two)[which * (CHUNKS // UNITS) : (which + 1) * (CHUNKS // UNITS)]
        waits = [s[i - 1] for i, s in enumerate(reversed(steps), 1) if i <= len(s)] if STEPS else []
        operand = tie(full, *waits) if waits else full
        keep, send = call(
            functools.partial(pair_kernel, members, which * (size // 2), early),
            [((2, half, per, size), F32)] * 2,
            [a, sibling, *some, operand],
            16,
            [pltpu.VMEM((2, size, freq), BF16), pltpu.VMEM((2, size // LANES, rows, LANES), F32)],
        )
        piece, new = reduce(keep, send, 2)
        pieces.append(piece)
        steps.append(new)

    early = [v for piece in pieces[:-1] for v in piece]
    (early_home,) = call(home_kernel, [((2 * UNITS - 1, per, size), F32)], early, 8)
    (late_home,) = call(home_kernel, [((1, per, size), F32)], pieces[-1], 8)
    sums = [v for piece in pieces for v in piece]
    operands = [pair_live, own_keep, own_got, *sums, exchange(early_home, 1), exchange(late_home, 1)]
    (out,) = call(
        functools.partial(final_kernel, factor),
        [((2 * PAIRS * per, 2 * block), F32)],
        operands,
        12,
        specs=[SMEM] + [VMEM] * (len(operands) - 1),
    )
    return out.reshape(block // members, channels, PAIRS, 2, 2 * block)


def solution(mesh):
    return jax.shard_map(
        per_device,
        mesh=mesh,
        in_specs=(P("stn", None, "seg", None, None), P("stn", "seg"), P("stn", None)),
        out_specs=P(("stn", "seg"), None, None, None, None),
        check_vma=False,
    )
```

```python
import functools
import math

import jax
import jax.numpy as jnp
from jax import lax
from jax.experimental import pallas as pl
from jax.experimental.pallas import tpu as pltpu
from jax.sharding import PartitionSpec as P

PAIRS = 5
CHUNKS = 4
ORDER = ("F0", "F1", "U", "F2", "F3", "X0", "X1", "F0F1", "X2", "X0X1", "X3", "F2F3", "X2X3")
TIES = {
    "F0F1b": ("X1",),
    "F2": ("Ua",),
    "F2F3": ("F0F1b",),
    "F3": ("F1", "S"),
    "X0": ("S", "Ua"),
    "X0X1": ("F0F1k", "F3", "Ub"),
    "X0X1b": ("F3",),
    "X2": ("F0F1k",),
    "X2X3": ("X0X1a",),
    "X3": ("F0F1a", "Ub", "X1"),
}
COST = None
LANES = 128
VMEM = pl.BlockSpec(memory_space=pltpu.VMEM)
HBM = pl.BlockSpec(memory_space=pltpu.HBM)
SMEM = pl.BlockSpec(memory_space=pltpu.SMEM)
F32 = jnp.float32
BF16 = jnp.bfloat16


def params(mib):
    return pltpu.CompilerParams(vmem_limit_bytes=mib * 2**20)


def iota(shape, dim):
    return lax.broadcasted_iota(jnp.int32, shape, dim)


def dot_t(a, b):
    return lax.dot_general(a, b, (((1,), (1,)), ((), ())), preferred_element_type=F32)


def extract_kernel(x_hbm, valid_hbm, full_ref, row_ref, *rest):
    *chunk_refs, buf, valid_buf, sems = rest
    copy = pltpu.make_async_copy(x_hbm.at[:, 2:4], buf, sems.at[0])
    copy.start()
    small = pltpu.make_async_copy(valid_hbm, valid_buf, sems.at[1])
    small.start()
    block = buf.shape[0]
    rows = 4 * block
    half = rows // 2
    spread = (iota((block, rows), 1) // 4 == iota((block, rows), 0)).astype(BF16)
    to, frm = iota((rows, rows), 0), iota((rows, rows), 1)
    source = jnp.where(to < half, 2 * to, 2 * (to - half) + 1)
    small.wait()
    valid = jnp.broadcast_to(valid_buf[...], row_ref.shape).astype(F32).astype(BF16)
    row_ref[...] = valid
    valid = jnp.dot(valid, spread, preferred_element_type=F32)[:1]
    pick = jnp.where(frm == source, jnp.broadcast_to(valid, (rows, rows)), 0.0).astype(BF16)
    copy.wait()
    full = jnp.dot(pick, buf[...].reshape(rows, buf.shape[-1]), preferred_element_type=F32).astype(BF16)
    full_ref[...] = full
    width = half // CHUNKS
    for k, chunk_ref in enumerate(chunk_refs):
        for part in range(2):
            at = part * half + k * width
            chunk_ref[part * width : (part + 1) * width] = full[at : at + width]


def store_tiles(g_ref, value):
    for tile in range(g_ref.shape[0]):
        g_ref[tile] = value[:, tile * LANES : (tile + 1) * LANES]


def combine(even, odd, span):
    part = iota((1, LANES), 1) // span % 2
    swapped = pltpu.roll(odd, span, 1)
    if 2 * span < LANES:
        swapped = jnp.where(part == 0, pltpu.roll(odd, LANES - span, 1), swapped)
    return swapped + jnp.where(part == 0, 1.0, -1.0) * even


def scatter(g_ref, out_keep, out_send, seg, members, finish):
    rows = g_ref.shape[-2] // members
    for slot in range(members):
        at = pl.multiple_of((seg ^ slot) * rows, 8)
        finish(
            [g_ref[t, pl.ds(at, rows // 2, stride=2), :] for t in range(g_ref.shape[0])],
            [g_ref[t, pl.ds(at + 1, rows // 2, stride=2), :] for t in range(g_ref.shape[0])],
            out_send if slot % 2 else out_keep,
            slot // 2,
        )


def own_kernel(members, x_ref, valid_ref, full_ref, a_ref, keep_ref, send_ref, g_ref):
    block = x_ref.shape[0]
    rows = a_ref.shape[0]
    pick = (iota((rows, block), 0) // (rows // block) == iota((rows, block), 1)).astype(BF16)
    valid = dot_t(pick, valid_ref[...])[:, :1].astype(BF16)
    a_ref[...] = x_ref[...].reshape(a_ref.shape) * valid
    store_tiles(g_ref, dot_t(a_ref[...], full_ref[...]))

    def finish(even, odd, out, slot):
        out[slot, :, :LANES] = even[0] + odd[1]
        out[slot, :, LANES:] = odd[0] - even[1]

    scatter(g_ref, keep_ref, send_ref, lax.axis_index("seg"), members, finish)


def place(index):
    return (lax.axis_index("stn") >> index) & 1 == 1


def choose_kernel(own_ref, four_ref, out_ref):
    odd = place(1)

    @pl.when(odd)
    def _():
        out_ref[...] = four_ref[...]

    @pl.when(jnp.logical_not(odd))
    def _():
        out_ref[...] = own_ref[...]


def unit_kernel(members, kinds, a_ref, sib_ref, *refs):
    count = len(kinds)
    piece_refs, own_refs = refs[:count], refs[count : 2 * count]
    _, keep_ref, send_ref, b_ref, g_ref = refs[2 * count :]
    width = piece_refs[0].shape[0] // 2
    second = place(0)

    def fill(which, i, ref):
        for part in range(2):
            to = (part * count + i) * width
            b_ref[which, to : to + width] = ref[part * width : (part + 1) * width]

    for i, kind in enumerate(kinds):
        fill(0, i, piece_refs[i])
        if kind == "F":
            pl.when(second)(functools.partial(fill, 1, i, piece_refs[i]))
            pl.when(jnp.logical_not(second))(functools.partial(fill, 1, i, own_refs[i]))
        else:
            fill(1, i, piece_refs[i])
    mine, theirs = dot_t(a_ref[...], b_ref[0]), dot_t(sib_ref[...], b_ref[1])
    store_tiles(g_ref, jnp.concatenate([mine, theirs], axis=1))

    def finish(even, odd, out, slot):
        for t in range(len(even)):
            out[t, slot] = combine(even[t], odd[t], count * width)

    scatter(g_ref, keep_ref, send_ref, lax.axis_index("seg"), members, finish)


def add_kernel(keep_ref, got_ref, new_keep_ref, new_send_ref):
    for slot in range(keep_ref.shape[0]):
        out = new_send_ref if slot % 2 else new_keep_ref
        out[slot // 2] = keep_ref[slot] + got_ref[slot]


def home_kernel(*refs):
    *in_refs, out_ref = refs
    for k in range(out_ref.shape[0]):
        last = in_refs[2 * k].shape[0] - 1
        out_ref[k] = in_refs[2 * k][last] + in_refs[2 * k + 1][last]


def final_kernel(factor, units, live_ref, *refs):
    own_keep_ref, own_got_ref, *in_refs, early_ref, late_ref, out_ref = refs
    own = own_keep_ref[...] + own_got_ref[...]
    second = jnp.broadcast_to(lax.axis_index("stn") & 1, own[:, :LANES].shape) == 1
    theirs = [r[i] for r in (early_ref, late_ref) for i in range(r.shape[0])]
    width = LANES // CHUNKS
    columns = {}
    for u, unit in enumerate(units):
        tiles = in_refs[2 * u].shape[0]
        mine = in_refs[2 * u][0] + in_refs[2 * u + 1][0]
        for i, (kind, k) in enumerate(unit):
            for part in range(2):
                at = (part * len(unit) + i) * width
                columns[kind, k, part] = mine[:, at : at + width]
                at += LANES // 2 if tiles == 1 else 0
                columns[kind + "s", k, part] = theirs[u][:, at : at + width]
    rows = out_ref.shape[0] // (2 * PAIRS)

    def joined(kind, part):
        return jnp.concatenate([columns[kind, k, part] for k in range(CHUNKS)], axis=1)

    for part in range(2):
        four, two = joined("Fs", part), joined("Xs", part)
        values = [
            own[:, part * LANES : (part + 1) * LANES],
            jnp.where(second, four, two),
            joined("X", part),
            jnp.where(second, two, four),
            joined("F", part),
        ]
        for offset, value in enumerate(values):
            scale = live_ref[0, offset].astype(F32) * factor
            out_ref[pl.ds(2 * offset + part, rows, stride=2 * PAIRS), :] = value * scale


def tie(values, *others):
    return lax.optimization_barrier((values, others))[0] if others else values


def per_device(spectra, segment_valid, pair_live):
    block, channels, seg_local, _, freq = spectra.shape
    blocks, members = lax.axis_size("stn"), lax.axis_size("seg")
    factor = 1.0 / math.sqrt(seg_local * members * freq)
    rows, per, half = 2 * block * channels, block * channels // members, members // 2
    width = 2 * block // CHUNKS
    ids = range(blocks)

    def call(kernel, outs, operands, mib, scratch=(), specs=None, cost=COST):
        return pl.pallas_call(
            kernel,
            in_specs=specs or [VMEM] * len(operands),
            out_specs=[VMEM] * len(outs),
            out_shape=[jax.ShapeDtypeStruct(*out) for out in outs],
            scratch_shapes=list(scratch),
            compiler_params=params(mib),
            cost_estimate=cost and pl.CostEstimate(flops=cost, bytes_accessed=cost, transcendentals=0),
        )(*operands)

    full, valid, *own = call(
        extract_kernel,
        [((4 * block, freq), BF16), ((8, block), BF16)] + [((2 * width, freq), BF16)] * CHUNKS,
        [pltpu.with_memory_space_constraint(v, pltpu.HBM) for v in (spectra, segment_valid.reshape(1, block))],
        12,
        [
            pltpu.VMEM((block, 2, 1, 2, freq), BF16),
            pltpu.VMEM((1, block), jnp.int32),
            pltpu.SemaphoreType.DMA((2,)),
        ],
        [HBM] * 2,
    )

    def exchange(c, distance):
        return lax.ppermute(c, "stn", [(i ^ distance, i) for i in ids])

    def halve(keep, send, distance, kinds):
        got = lax.ppermute(send, "seg", [(i ^ distance, i) for i in range(members)])
        lead = (kinds,) if kinds else ()
        slots = keep.shape[len(lead)]
        if slots == 1:
            return keep.reshape(*lead, *keep.shape[-2:]), got.reshape(*lead, *keep.shape[-2:])
        shape = (max(kinds, 1) * slots // 2, *keep.shape[-2:])
        new = call(add_kernel, [(shape, F32)] * 2, [v.reshape(-1, *shape[1:]) for v in (keep, got)], 8)
        return [v.reshape(*lead, slots // 2, *shape[1:]) for v in new]

    def reduce(keep, send, kinds, name):
        distance = 1
        while distance < members:
            if 2 * distance == members:
                send = tie(send, *after(name + "b"))
            keep, send = halve(keep, send, distance, kinds)
            done[name + ("a" if distance == 1 else "b")] = keep if 2 * distance < members else send
            distance *= 2
        return keep, send

    a, keep, send = call(
        functools.partial(own_kernel, members),
        [((rows, freq), BF16)] + [((half, per, 4 * block), F32)] * 2,
        [spectra, valid, full],
        16,
        [pltpu.VMEM((4 * block // LANES, rows, LANES), F32)],
    )
    sibling = exchange(a, 1)
    done = {}

    def after(name):
        return [done[n] for n in TIES.get(name, ())]

    sibling = exchange(tie(a, *after("S")), 1)
    done["S"] = sibling

    def four_of(k):
        value = tie(own[k], *after("F%d" % k))
        done["F%d" % k] = lax.ppermute(value, "stn", [((i - 4) % blocks, i) for i in ids])
        return done["F%d" % k]

    def two_of(k):
        value = tie(own[k], *after("X%d" % k))
        (c,) = call(choose_kernel, [((2 * width, freq), BF16)], [value, four[k]], 8)
        done["X%d" % k] = exchange(c, 2)
        return done["X%d" % k]

    def unit(name):
        pieces = [(name[i], int(name[i + 1])) for i in range(0, len(name), 2)]
        columns = 2 * width * len(pieces)
        tiles = max(1, 2 * columns // LANES)
        keep, send = call(
            functools.partial(unit_kernel, members, [p[0] for p in pieces]),
            [((tiles, half, per, LANES), F32)] * 2,
            [a, sibling]
            + [(four if kind == "F" else two)[k] for kind, k in pieces]
            + [own[k] for _, k in pieces]
            + [tie(valid, *after(name))],
            16,
            [pltpu.VMEM((2, columns, freq), BF16), pltpu.VMEM((tiles, rows, LANES), F32)],
        )
        done[name + "k"] = keep
        return pieces, reduce(keep, send, tiles, name)

    four, two = [], []
    units = []
    for name in ORDER:
        if name == "U":
            own_keep, own_got = reduce(keep, send, 0, "U")
        elif len(name) == 2 and name[0] == "F" and len(four) <= int(name[1]):
            four.append(four_of(int(name[1])))
        elif len(name) == 2 and name[0] == "X" and len(two) <= int(name[1]):
            two.append(two_of(int(name[1])))
        else:
            units.append(unit(name))
    pieces = [piece for _, piece in units]
    units = [names for names, _ in units]
    early = [v for piece in pieces[:-1] for v in piece]
    (early_home,) = call(home_kernel, [((len(pieces) - 1, per, LANES), F32)], early, 8)
    (late_home,) = call(home_kernel, [((1, per, LANES), F32)], pieces[-1], 8)
    sums = [v for piece in pieces for v in piece]
    operands = [pair_live, own_keep, own_got, *sums, exchange(early_home, 1), exchange(late_home, 1)]
    (out,) = call(
        functools.partial(final_kernel, factor, units),
        [((2 * PAIRS * per, 2 * block), F32)],
        operands,
        12,
        specs=[SMEM] + [VMEM] * (len(operands) - 1),
    )
    return out.reshape(block // members, channels, PAIRS, 2, 2 * block)


def solution(mesh):
    return jax.shard_map(
        per_device,
        mesh=mesh,
        in_specs=(P("stn", None, "seg", None, None), P("stn", "seg"), P("stn", None)),
        out_specs=P(("stn", "seg"), None, None, None, None),
        check_vma=False,
    )
```

```python
import functools
import math

import jax
import jax.numpy as jnp
from jax import lax
from jax.experimental import pallas as pl
from jax.experimental.pallas import tpu as pltpu
from jax.sharding import PartitionSpec as P

PAIRS = 5
CHUNKS = 4
STEPS = 5
ORDER = ("F0", "F1", "U", "F2", "F3", "X0", "X1", "F0F1", "X2", "X0X1", "X3", "F2F3", "X2X3")
TIES = {
    "F0F1b": ("X1",),
    "F2": ("Ua",),
    "F2F3": ("F0F1b",),
    "F3": ("F1", "S"),
    "X0": ("S", "Ua"),
    "X0X1": ("F0F1k", "F2", "Ub"),
    "X0X1b": ("F3",),
    "X2": ("F0F1k",),
    "X2X3": ("X0X1a",),
    "X3": ("F0F1a", "Ub", "X0X1k"),
}
LANES = 128
VMEM = pl.BlockSpec(memory_space=pltpu.VMEM)
HBM = pl.BlockSpec(memory_space=pltpu.HBM)
SMEM = pl.BlockSpec(memory_space=pltpu.SMEM)
F32 = jnp.float32
BF16 = jnp.bfloat16


def params(mib):
    return pltpu.CompilerParams(vmem_limit_bytes=mib * 2**20)


def iota(shape, dim):
    return lax.broadcasted_iota(jnp.int32, shape, dim)


def dot_t(a, b):
    return lax.dot_general(a, b, (((1,), (1,)), ((), ())), preferred_element_type=F32)


def store_tiles(g_ref, value):
    for tile in range(g_ref.shape[0]):
        g_ref[tile] = value[:, tile * LANES : (tile + 1) * LANES]


def combine(even, odd, span):
    part = iota((1, LANES), 1) // span % 2
    swapped = pltpu.roll(odd, span, 1)
    if 2 * span < LANES:
        swapped = jnp.where(part == 0, pltpu.roll(odd, LANES - span, 1), swapped)
    return swapped + jnp.where(part == 0, 1.0, -1.0) * even


def scatter(g_ref, out_keep, out_send, seg, members, finish):
    rows = g_ref.shape[-2] // members
    for slot in range(members):
        at = pl.multiple_of((seg ^ slot) * rows, 8)
        finish(
            [g_ref[t, pl.ds(at, rows // 2, stride=2), :] for t in range(g_ref.shape[0])],
            [g_ref[t, pl.ds(at + 1, rows // 2, stride=2), :] for t in range(g_ref.shape[0])],
            out_send if slot % 2 else out_keep,
            slot // 2,
        )


def first_kernel(members, x_hbm, valid_hbm, *refs):
    row_ref, *chunk_refs, a_ref, keep_ref, send_ref, buf, valid_buf, b_ref, g_ref, sems = refs
    copies = [
        pltpu.make_async_copy(valid_hbm, valid_buf, sems.at[0]),
        pltpu.make_async_copy(x_hbm.at[:, 2:4], buf.at[:, 2:4], sems.at[1]),
        pltpu.make_async_copy(x_hbm.at[:, :2], buf.at[:, :2], sems.at[2]),
        pltpu.make_async_copy(x_hbm.at[:, 4:], buf.at[:, 4:], sems.at[3]),
    ]
    for copy in copies:
        copy.start()
    block = buf.shape[0]
    stations = block // len(chunk_refs)
    rows = 4 * stations
    half = rows // 2
    station, lane = iota((block, rows), 0), iota((block, rows), 1)
    to, frm = iota((rows, rows), 0), iota((rows, rows), 1)
    source = jnp.where(to < half, 2 * to, 2 * (to - half) + 1)
    copies[0].wait()
    valid = jnp.broadcast_to(valid_buf[...], row_ref.shape).astype(F32).astype(BF16)
    row_ref[...] = valid
    picks = []
    for k in range(len(chunk_refs)):
        spread = (lane // 4 + k * stations == station).astype(BF16)
        mask = jnp.dot(valid, spread, preferred_element_type=F32)[:1]
        picks.append(jnp.where(frm == source, jnp.broadcast_to(mask, (rows, rows)), 0.0).astype(BF16))
    pick = (iota((a_ref.shape[0], block), 0) // (a_ref.shape[0] // block) == iota((a_ref.shape[0], block), 1)).astype(BF16)
    mask = dot_t(pick, valid)[:, :1].astype(BF16)
    copies[1].wait()
    for k, chunk_ref in enumerate(chunk_refs):
        some = buf[k * stations : (k + 1) * stations, 2:4].reshape(rows, buf.shape[-1])
        chunk = jnp.dot(picks[k], some, preferred_element_type=F32).astype(BF16)
        chunk_ref[...] = chunk
        for part in range(2):
            at = part * b_ref.shape[0] // 2 + k * half
            b_ref[at : at + half] = chunk[part * half : (part + 1) * half]
    copies[2].wait()
    copies[3].wait()
    a_ref[...] = buf[...].reshape(a_ref.shape) * mask
    store_tiles(g_ref, dot_t(a_ref[...], b_ref[...]))

    def finish(even, odd, out, slot):
        out[slot, :, :LANES] = even[0] + odd[1]
        out[slot, :, LANES:] = odd[0] - even[1]

    scatter(g_ref, keep_ref, send_ref, lax.axis_index("seg"), members, finish)


def place(index):
    return (lax.axis_index("stn") >> index) & 1 == 1


def choose_kernel(own_ref, four_ref, out_ref):
    odd = place(1)

    @pl.when(odd)
    def _():
        out_ref[...] = four_ref[...]

    @pl.when(jnp.logical_not(odd))
    def _():
        out_ref[...] = own_ref[...]


def unit_kernel(members, kinds, a_ref, sib_ref, *refs):
    count = len(kinds)
    piece_refs, own_refs = refs[:count], refs[count : 2 * count]
    _, keep_ref, send_ref, b_ref, g_ref = refs[2 * count :]
    width = piece_refs[0].shape[0] // 2
    second = place(0)

    def fill(which, i, ref):
        for part in range(2):
            to = (part * count + i) * width
            b_ref[which, to : to + width] = ref[part * width : (part + 1) * width]

    for i, kind in enumerate(kinds):
        fill(0, i, piece_refs[i])
        if kind == "F":
            pl.when(second)(functools.partial(fill, 1, i, piece_refs[i]))
            pl.when(jnp.logical_not(second))(functools.partial(fill, 1, i, own_refs[i]))
        else:
            fill(1, i, piece_refs[i])
    mine, theirs = dot_t(a_ref[...], b_ref[0]), dot_t(sib_ref[...], b_ref[1])
    store_tiles(g_ref, jnp.concatenate([mine, theirs], axis=1))

    def finish(even, odd, out, slot):
        for t in range(len(even)):
            out[t, slot] = combine(even[t], odd[t], count * width)

    scatter(g_ref, keep_ref, send_ref, lax.axis_index("seg"), members, finish)


def add_kernel(keep_ref, got_ref, new_keep_ref, new_send_ref):
    for slot in range(keep_ref.shape[0]):
        out = new_send_ref if slot % 2 else new_keep_ref
        out[slot // 2] = keep_ref[slot] + got_ref[slot]


def home_kernel(*refs):
    *in_refs, out_ref = refs
    for k in range(out_ref.shape[0]):
        last = in_refs[2 * k].shape[0] - 1
        out_ref[k] = in_refs[2 * k][last] + in_refs[2 * k + 1][last]


def final_kernel(factor, units, live_ref, *refs):
    own_keep_ref, own_got_ref, *in_refs, early_ref, late_ref, out_hbm, out_ref, sems = refs
    places = [(r, i) for r in (early_ref, late_ref) for i in range(r.shape[0])]
    width = LANES // CHUNKS
    steps = sems.shape[0]
    rows = out_ref.shape[0] // (2 * PAIRS * steps)
    copies = []
    for step in range(steps):
        some = pl.ds(step * rows, rows)
        own = own_keep_ref[some, :] + own_got_ref[some, :]
        second = jnp.broadcast_to(lax.axis_index("stn") & 1, own[:, :LANES].shape) == 1
        columns = {}
        for u, unit in enumerate(units):
            tiles = in_refs[2 * u].shape[0]
            mine = in_refs[2 * u][0, some, :] + in_refs[2 * u + 1][0, some, :]
            theirs = places[u][0][places[u][1], some, :]
            for i, (kind, k) in enumerate(unit):
                for part in range(2):
                    at = (part * len(unit) + i) * width
                    columns[kind, k, part] = mine[:, at : at + width]
                    at += LANES // 2 if tiles == 1 else 0
                    columns[kind + "s", k, part] = theirs[:, at : at + width]
        for part in range(2):
            four, two, mine_two, mine_four = (
                jnp.concatenate([columns[kind, k, part] for k in range(CHUNKS)], axis=1)
                for kind in ("Fs", "Xs", "X", "F")
            )
            values = [
                own[:, part * LANES : (part + 1) * LANES],
                jnp.where(second, four, two),
                mine_two,
                jnp.where(second, two, four),
                mine_four,
            ]
            for offset, value in enumerate(values):
                scale = live_ref[0, offset].astype(F32) * factor
                to = step * rows * 2 * PAIRS + 2 * offset + part
                out_ref[pl.ds(to, rows, stride=2 * PAIRS), :] = value * scale
        slab = pl.ds(step * rows * 2 * PAIRS, rows * 2 * PAIRS)
        copies.append(pltpu.make_async_copy(out_ref.at[slab], out_hbm.at[slab], sems.at[step]))
        copies[-1].start()
    for copy in copies:
        copy.wait()


def tie(values, *others):
    return lax.optimization_barrier((values, others))[0] if others else values


def per_device(spectra, segment_valid, pair_live):
    block, channels, seg_local, _, freq = spectra.shape
    blocks, members = lax.axis_size("stn"), lax.axis_size("seg")
    factor = 1.0 / math.sqrt(seg_local * members * freq)
    rows, per, half = 2 * block * channels, block * channels // members, members // 2
    width = 2 * block // CHUNKS
    ids = range(blocks)

    def call(kernel, outs, operands, mib, scratch=(), specs=None, out_spec=VMEM):
        return pl.pallas_call(
            kernel,
            in_specs=specs or [VMEM] * len(operands),
            out_specs=[out_spec] * len(outs),
            out_shape=[jax.ShapeDtypeStruct(*out) for out in outs],
            scratch_shapes=list(scratch),
            compiler_params=params(mib),
        )(*operands)

    valid, *own, a, keep, send = call(
        functools.partial(first_kernel, members),
        [((8, block), BF16)]
        + [((2 * width, freq), BF16)] * CHUNKS
        + [((rows, freq), BF16)]
        + [((half, per, 4 * block), F32)] * 2,
        [pltpu.with_memory_space_constraint(v, pltpu.HBM) for v in (spectra, segment_valid.reshape(1, block))],
        16,
        [
            pltpu.VMEM((block, channels, 1, 2, freq), BF16),
            pltpu.VMEM((1, block), jnp.int32),
            pltpu.VMEM((4 * block, freq), BF16),
            pltpu.VMEM((4 * block // LANES, rows, LANES), F32),
            pltpu.SemaphoreType.DMA((4,)),
        ],
        [HBM] * 2,
    )

    def exchange(c, distance):
        return lax.ppermute(c, "stn", [(i ^ distance, i) for i in ids])

    def halve(keep, send, distance, kinds):
        got = lax.ppermute(send, "seg", [(i ^ distance, i) for i in range(members)])
        lead = (kinds,) if kinds else ()
        slots = keep.shape[len(lead)]
        if slots == 1:
            return keep.reshape(*lead, *keep.shape[-2:]), got.reshape(*lead, *keep.shape[-2:])
        shape = (max(kinds, 1) * slots // 2, *keep.shape[-2:])
        new = call(add_kernel, [(shape, F32)] * 2, [v.reshape(-1, *shape[1:]) for v in (keep, got)], 8)
        return [v.reshape(*lead, slots // 2, *shape[1:]) for v in new]

    def reduce(keep, send, kinds, name):
        distance = 1
        while distance < members:
            if 2 * distance == members:
                send = tie(send, *after(name + "b"))
            keep, send = halve(keep, send, distance, kinds)
            done[name + ("a" if distance == 1 else "b")] = keep if 2 * distance < members else send
            distance *= 2
        return keep, send

    done = {}

    def after(name):
        return [done[n] for n in TIES.get(name, ())]

    sibling = exchange(tie(a, *after("S")), 1)
    done["S"] = sibling

    def four_of(k):
        value = tie(own[k], *after("F%d" % k))
        done["F%d" % k] = lax.ppermute(value, "stn", [((i - 4) % blocks, i) for i in ids])
        return done["F%d" % k]

    def two_of(k):
        value = tie(own[k], *after("X%d" % k))
        (c,) = call(choose_kernel, [((2 * width, freq), BF16)], [value, four[k]], 8)
        done["X%d" % k] = exchange(c, 2)
        return done["X%d" % k]

    def unit(name):
        pieces = [(name[i], int(name[i + 1])) for i in range(0, len(name), 2)]
        columns = 2 * width * len(pieces)
        tiles = max(1, 2 * columns // LANES)
        keep, send = call(
            functools.partial(unit_kernel, members, [p[0] for p in pieces]),
            [((tiles, half, per, LANES), F32)] * 2,
            [a, sibling]
            + [(four if kind == "F" else two)[k] for kind, k in pieces]
            + [own[k] for _, k in pieces]
            + [tie(valid, *after(name))],
            16,
            [pltpu.VMEM((2, columns, freq), BF16), pltpu.VMEM((tiles, rows, LANES), F32)],
        )
        done[name + "k"] = keep
        return pieces, reduce(keep, send, tiles, name)

    four, two = [], []
    units = []
    for name in ORDER:
        if name == "U":
            own_keep, own_got = reduce(keep, send, 0, "U")
        elif len(name) == 2 and name[0] == "F" and len(four) <= int(name[1]):
            four.append(four_of(int(name[1])))
        elif len(name) == 2 and name[0] == "X" and len(two) <= int(name[1]):
            two.append(two_of(int(name[1])))
        else:
            units.append(unit(name))
    pieces = [piece for _, piece in units]
    units = [names for names, _ in units]
    early = [v for piece in pieces[:-1] for v in piece]
    (early_home,) = call(home_kernel, [((len(pieces) - 1, per, LANES), F32)], early, 8)
    (late_home,) = call(home_kernel, [((1, per, LANES), F32)], pieces[-1], 8)
    sums = [v for piece in pieces for v in piece]
    operands = [pair_live, own_keep, own_got, *sums, exchange(early_home, 1), exchange(late_home, 1)]
    (out,) = call(
        functools.partial(final_kernel, factor, units),
        [((2 * PAIRS * per, 2 * block), F32)],
        operands,
        12,
        [
            pltpu.VMEM((2 * PAIRS * per, 2 * block), F32),
            pltpu.SemaphoreType.DMA((STEPS if per % (8 * STEPS) == 0 else 1,)),
        ],
        [SMEM] + [VMEM] * (len(operands) - 1),
        HBM,
    )
    return out.reshape(block // members, channels, PAIRS, 2, 2 * block)


def solution(mesh):
    return jax.shard_map(
        per_device,
        mesh=mesh,
        in_specs=(P("stn", None, "seg", None, None), P("stn", "seg"), P("stn", None)),
        out_specs=P(("stn", "seg"), None, None, None, None),
        check_vma=False,
    )
```

```python
import functools
import math

import jax
import jax.numpy as jnp
from jax import lax
from jax.experimental import pallas as pl
from jax.experimental.pallas import tpu as pltpu
from jax.sharding import PartitionSpec as P

PAIRS = 5
CHUNKS = 4
STEPS = 5
ORDER = ("F0", "F1", "U", "F2", "F3", "X0", "F0F1", "X1", "F2X0", "X2", "F3X1", "X3", "X2X3")
TIES = {
    "F2": ("S",),
    "F2X0": ("F0F1a", "Ub"),
    "F3": ("F0", "S", "Ub"),
    "F3X1": ("F2X0a",),
    "X0": ("S", "Ua"),
    "X1": ("F0F1k",),
    "X2": ("F0F1a", "Ua"),
    "X2X3": ("F0F1b",),
    "X3": ("F2X0k",),
}
JOINT = ("F2X0", "F3X1")
LANES = 128
VMEM = pl.BlockSpec(memory_space=pltpu.VMEM)
HBM = pl.BlockSpec(memory_space=pltpu.HBM)
SMEM = pl.BlockSpec(memory_space=pltpu.SMEM)
F32 = jnp.float32
BF16 = jnp.bfloat16


def params(mib):
    return pltpu.CompilerParams(vmem_limit_bytes=mib * 2**20)


def iota(shape, dim):
    return lax.broadcasted_iota(jnp.int32, shape, dim)


def dot_t(a, b):
    return lax.dot_general(a, b, (((1,), (1,)), ((), ())), preferred_element_type=F32)


def store_tiles(g_ref, value):
    for tile in range(g_ref.shape[0]):
        g_ref[tile] = value[:, tile * LANES : (tile + 1) * LANES]


def combine(even, odd, span):
    part = iota((1, LANES), 1) // span % 2
    swapped = pltpu.roll(odd, span, 1)
    if 2 * span < LANES:
        swapped = jnp.where(part == 0, pltpu.roll(odd, LANES - span, 1), swapped)
    return swapped + jnp.where(part == 0, 1.0, -1.0) * even


def scatter(g_ref, out_keep, out_send, seg, members, finish):
    rows = g_ref.shape[-2] // members
    for slot in range(members):
        at = pl.multiple_of((seg ^ slot) * rows, 8)
        finish(
            [g_ref[t, pl.ds(at, rows // 2, stride=2), :] for t in range(g_ref.shape[0])],
            [g_ref[t, pl.ds(at + 1, rows // 2, stride=2), :] for t in range(g_ref.shape[0])],
            out_send if slot % 2 else out_keep,
            slot // 2,
        )


def first_kernel(members, x_hbm, valid_hbm, *refs):
    row_ref, *chunk_refs, a_ref, keep_ref, send_ref, buf, valid_buf, b_ref, g_ref, sems = refs
    copies = [
        pltpu.make_async_copy(valid_hbm, valid_buf, sems.at[0]),
        pltpu.make_async_copy(x_hbm.at[:, 2:4], buf.at[:, 2:4], sems.at[1]),
        pltpu.make_async_copy(x_hbm.at[:, :2], buf.at[:, :2], sems.at[2]),
        pltpu.make_async_copy(x_hbm.at[:, 4:], buf.at[:, 4:], sems.at[3]),
    ]
    for copy in copies:
        copy.start()
    block = buf.shape[0]
    stations = block // len(chunk_refs)
    rows = 4 * stations
    half = rows // 2
    station, lane = iota((block, rows), 0), iota((block, rows), 1)
    to, frm = iota((rows, rows), 0), iota((rows, rows), 1)
    source = jnp.where(to < half, 2 * to, 2 * (to - half) + 1)
    copies[0].wait()
    valid = jnp.broadcast_to(valid_buf[...], row_ref.shape).astype(F32).astype(BF16)
    row_ref[...] = valid
    picks = []
    for k in range(len(chunk_refs)):
        spread = (lane // 4 + k * stations == station).astype(BF16)
        mask = jnp.dot(valid, spread, preferred_element_type=F32)[:1]
        picks.append(jnp.where(frm == source, jnp.broadcast_to(mask, (rows, rows)), 0.0).astype(BF16))
    pick = (iota((a_ref.shape[0], block), 0) // (a_ref.shape[0] // block) == iota((a_ref.shape[0], block), 1)).astype(BF16)
    mask = dot_t(pick, valid)[:, :1].astype(BF16)
    copies[1].wait()
    for k, chunk_ref in enumerate(chunk_refs):
        some = buf[k * stations : (k + 1) * stations, 2:4].reshape(rows, buf.shape[-1])
        chunk = jnp.dot(picks[k], some, preferred_element_type=F32).astype(BF16)
        chunk_ref[...] = chunk
        for part in range(2):
            at = part * b_ref.shape[0] // 2 + k * half
            b_ref[at : at + half] = chunk[part * half : (part + 1) * half]
    copies[2].wait()
    copies[3].wait()
    a_ref[...] = buf[...].reshape(a_ref.shape) * mask
    store_tiles(g_ref, dot_t(a_ref[...], b_ref[...]))

    def finish(even, odd, out, slot):
        out[slot, :, :LANES] = even[0] + odd[1]
        out[slot, :, LANES:] = odd[0] - even[1]

    scatter(g_ref, keep_ref, send_ref, lax.axis_index("seg"), members, finish)


def place(index):
    return (lax.axis_index("stn") >> index) & 1 == 1


def choose_kernel(own_ref, four_ref, out_ref):
    odd = place(1)

    @pl.when(odd)
    def _():
        out_ref[...] = four_ref[...]

    @pl.when(jnp.logical_not(odd))
    def _():
        out_ref[...] = own_ref[...]


def unit_kernel(members, kinds, a_ref, sib_ref, *refs):
    count = len(kinds)
    piece_refs, own_refs = refs[:count], refs[count : 2 * count]
    _, keep_ref, send_ref, b_ref, g_ref = refs[2 * count :]
    width = piece_refs[0].shape[0] // 2
    second = place(0)

    def fill(which, i, ref):
        for part in range(2):
            to = (part * count + i) * width
            b_ref[which, to : to + width] = ref[part * width : (part + 1) * width]

    for i, kind in enumerate(kinds):
        fill(0, i, piece_refs[i])
        if kind == "F":
            pl.when(second)(functools.partial(fill, 1, i, piece_refs[i]))
            pl.when(jnp.logical_not(second))(functools.partial(fill, 1, i, own_refs[i]))
        else:
            fill(1, i, piece_refs[i])
    mine, theirs = dot_t(a_ref[...], b_ref[0]), dot_t(sib_ref[...], b_ref[1])
    store_tiles(g_ref, jnp.concatenate([mine, theirs], axis=1))

    def finish(even, odd, out, slot):
        for t in range(len(even)):
            out[t, slot] = combine(even[t], odd[t], count * width)

    scatter(g_ref, keep_ref, send_ref, lax.axis_index("seg"), members, finish)


def add_kernel(keep_ref, got_ref, new_keep_ref, new_send_ref):
    for slot in range(keep_ref.shape[0]):
        out = new_send_ref if slot % 2 else new_keep_ref
        out[slot // 2] = keep_ref[slot] + got_ref[slot]


def joint_add_kernel(*refs):
    *in_refs, keep_ref, send_ref = refs
    for u in range(len(in_refs) // 2):
        for t in range(2):
            keep_ref[2 * u + t] = in_refs[2 * u][t, 0] + in_refs[2 * u + 1][t, 0]
            send_ref[2 * u + t] = in_refs[2 * u][t, 1] + in_refs[2 * u + 1][t, 1]


def home_kernel(bases, *refs):
    *in_refs, out_ref = refs
    for k, base in enumerate(bases):
        out_ref[k] = in_refs[2 * k][base + 1] + in_refs[2 * k + 1][base + 1]


def final_kernel(factor, units, bases, live_ref, *refs):
    own_keep_ref, own_got_ref, *in_refs, early_ref, late_ref, out_hbm, out_ref, sems = refs
    places = [(r, i) for r in (early_ref, late_ref) for i in range(r.shape[0])]
    width = LANES // CHUNKS
    steps = sems.shape[0]
    rows = out_ref.shape[0] // (2 * PAIRS * steps)
    copies = []
    for step in range(steps):
        some = pl.ds(step * rows, rows)
        own = own_keep_ref[some, :] + own_got_ref[some, :]
        second = jnp.broadcast_to(lax.axis_index("stn") & 1, own[:, :LANES].shape) == 1
        columns = {}
        for u, unit in enumerate(units):
            mine = in_refs[2 * u][bases[u], some, :] + in_refs[2 * u + 1][bases[u], some, :]
            theirs = places[u][0][places[u][1], some, :]
            for i, (kind, k) in enumerate(unit):
                for part in range(2):
                    at = (part * len(unit) + i) * width
                    columns[kind, k, part] = mine[:, at : at + width]
                    columns[kind + "s", k, part] = theirs[:, at : at + width]
        for part in range(2):
            four, two, mine_two, mine_four = (
                jnp.concatenate([columns[kind, k, part] for k in range(CHUNKS)], axis=1)
                for kind in ("Fs", "Xs", "X", "F")
            )
            values = [
                own[:, part * LANES : (part + 1) * LANES],
                jnp.where(second, four, two),
                mine_two,
                jnp.where(second, two, four),
                mine_four,
            ]
            for offset, value in enumerate(values):
                scale = live_ref[0, offset].astype(F32) * factor
                to = step * rows * 2 * PAIRS + 2 * offset + part
                out_ref[pl.ds(to, rows, stride=2 * PAIRS), :] = value * scale
        slab = pl.ds(step * rows * 2 * PAIRS, rows * 2 * PAIRS)
        copies.append(pltpu.make_async_copy(out_ref.at[slab], out_hbm.at[slab], sems.at[step]))
        copies[-1].start()
    for copy in copies:
        copy.wait()


def tie(values, *others):
    return lax.optimization_barrier((values, others))[0] if others else values


def per_device(spectra, segment_valid, pair_live):
    block, channels, seg_local, _, freq = spectra.shape
    blocks, members = lax.axis_size("stn"), lax.axis_size("seg")
    factor = 1.0 / math.sqrt(seg_local * members * freq)
    rows, per, half = 2 * block * channels, block * channels // members, members // 2
    width = 2 * block // CHUNKS
    ids = range(blocks)

    def call(kernel, outs, operands, mib, scratch=(), specs=None, out_spec=VMEM):
        return pl.pallas_call(
            kernel,
            in_specs=specs or [VMEM] * len(operands),
            out_specs=[out_spec] * len(outs),
            out_shape=[jax.ShapeDtypeStruct(*out) for out in outs],
            scratch_shapes=list(scratch),
            compiler_params=params(mib),
        )(*operands)

    valid, *own, a, keep, send = call(
        functools.partial(first_kernel, members),
        [((8, block), BF16)]
        + [((2 * width, freq), BF16)] * CHUNKS
        + [((rows, freq), BF16)]
        + [((half, per, 4 * block), F32)] * 2,
        [pltpu.with_memory_space_constraint(v, pltpu.HBM) for v in (spectra, segment_valid.reshape(1, block))],
        16,
        [
            pltpu.VMEM((block, channels, 1, 2, freq), BF16),
            pltpu.VMEM((1, block), jnp.int32),
            pltpu.VMEM((4 * block, freq), BF16),
            pltpu.VMEM((4 * block // LANES, rows, LANES), F32),
            pltpu.SemaphoreType.DMA((4,)),
        ],
        [HBM] * 2,
    )

    def exchange(c, distance):
        return lax.ppermute(c, "stn", [(i ^ distance, i) for i in ids])

    def halve(keep, send, distance, kinds):
        got = lax.ppermute(send, "seg", [(i ^ distance, i) for i in range(members)])
        lead = (kinds,) if kinds else ()
        slots = keep.shape[len(lead)]
        if slots == 1:
            return keep.reshape(*lead, *keep.shape[-2:]), got.reshape(*lead, *keep.shape[-2:])
        shape = (max(kinds, 1) * slots // 2, *keep.shape[-2:])
        new = call(add_kernel, [(shape, F32)] * 2, [v.reshape(-1, *shape[1:]) for v in (keep, got)], 8)
        return [v.reshape(*lead, slots // 2, *shape[1:]) for v in new]

    def reduce(keep, send, kinds, name):
        distance = 1
        while distance < members:
            if 2 * distance == members:
                send = tie(send, *after(name + "b"))
            keep, send = halve(keep, send, distance, kinds)
            done[name + ("a" if distance == 1 else "b")] = keep if 2 * distance < members else send
            distance *= 2
        return keep, send

    done = {}

    def after(name):
        return [done[n] for n in TIES.get(name, ())]

    sibling = exchange(tie(a, *after("S")), 1)
    done["S"] = sibling

    def four_of(k):
        value = tie(own[k], *after("F%d" % k))
        done["F%d" % k] = lax.ppermute(value, "stn", [((i - 4) % blocks, i) for i in ids])
        return done["F%d" % k]

    def two_of(k):
        value = tie(own[k], *after("X%d" % k))
        (c,) = call(choose_kernel, [((2 * width, freq), BF16)], [value, four[k]], 8)
        done["X%d" % k] = exchange(c, 2)
        return done["X%d" % k]

    def unit(name):
        pieces = [(name[i], int(name[i + 1])) for i in range(0, len(name), 2)]
        columns = 2 * width * len(pieces)
        tiles = max(1, 2 * columns // LANES)
        keep, send = call(
            functools.partial(unit_kernel, members, [p[0] for p in pieces]),
            [((tiles, half, per, LANES), F32)] * 2,
            [a, sibling]
            + [(four if kind == "F" else two)[k] for kind, k in pieces]
            + [own[k] for _, k in pieces]
            + [tie(valid, *after(name))],
            16,
            [pltpu.VMEM((2, columns, freq), BF16), pltpu.VMEM((tiles, rows, LANES), F32)],
        )
        done[name + "k"] = keep
        if name not in JOINT:
            return pieces, reduce(keep, send, tiles, name), 0
        distance = 1
        while 4 * distance < members:
            keep, send = halve(keep, send, distance, tiles)
            distance *= 2
        got = lax.ppermute(send, "seg", [(i ^ distance, i) for i in range(members)])
        done[name + "a"] = got
        held.extend([keep, got])
        if len(held) == 2 * len(JOINT):
            shape = (2 * len(JOINT), per, LANES)
            kept, sent = call(joint_add_kernel, [(shape, F32)] * 2, held, 8)
            distance = members // 2
            done["J"] = lax.ppermute(sent, "seg", [(i ^ distance, i) for i in range(members)])
            joint.extend([kept, done["J"]])
        return pieces, joint, 2 * (len(held) // 2 - 1)

    four, two, held, joint = [], [], [], []
    units = []
    for name in ORDER:
        if name == "U":
            own_keep, own_got = reduce(keep, send, 0, "U")
        elif len(name) == 2 and name[0] == "F" and len(four) <= int(name[1]):
            four.append(four_of(int(name[1])))
        elif len(name) == 2 and name[0] == "X" and len(two) <= int(name[1]):
            two.append(two_of(int(name[1])))
        else:
            units.append(unit(name))
    bases = [base for _, _, base in units]
    pieces = [piece for _, piece, _ in units]
    units = [names for names, _, _ in units]
    early = [v for piece in pieces[:-1] for v in piece]
    (early_home,) = call(functools.partial(home_kernel, bases[:-1]), [((len(pieces) - 1, per, LANES), F32)], early, 8)
    (late_home,) = call(functools.partial(home_kernel, bases[-1:]), [((1, per, LANES), F32)], pieces[-1], 8)
    sums = [v for piece in pieces for v in piece]
    operands = [pair_live, own_keep, own_got, *sums, exchange(early_home, 1), exchange(late_home, 1)]
    (out,) = call(
        functools.partial(final_kernel, factor, units, bases),
        [((2 * PAIRS * per, 2 * block), F32)],
        operands,
        12,
        [
            pltpu.VMEM((2 * PAIRS * per, 2 * block), F32),
            pltpu.SemaphoreType.DMA((STEPS if per % (8 * STEPS) == 0 else 1,)),
        ],
        [SMEM] + [VMEM] * (len(operands) - 1),
        HBM,
    )
    return out.reshape(block // members, channels, PAIRS, 2, 2 * block)


def solution(mesh):
    return jax.shard_map(
        per_device,
        mesh=mesh,
        in_specs=(P("stn", None, "seg", None, None), P("stn", "seg"), P("stn", None)),
        out_specs=P(("stn", "seg"), None, None, None, None),
        check_vma=False,
    )
```

```python
import functools
import math

import jax
import jax.numpy as jnp
from jax import lax
from jax.experimental import pallas as pl
from jax.experimental.pallas import tpu as pltpu
from jax.sharding import PartitionSpec as P

PAIRS = 5
CHUNKS = 4
STEPS = 5
ORDER = ("F0", "F1", "U", "F2", "F3", "X0", "F0F1", "X1", "F2X0", "X2", "F3X1", "X3", "X2X3")
TIES = {
    "F2": ("S",),
    "F2X0": ("F0F1a", "Ub"),
    "F3": ("F0", "S", "Ub"),
    "F3X1": ("F2X0a",),
    "X0": ("S", "Ua"),
    "X2": ("F0F1a", "Ua"),
    "X2X3": ("F0F1b",),
    "X3": ("F2X0k",),
}
JOINT = ("F2X0", "F3X1")
LANES = 128
VMEM = pl.BlockSpec(memory_space=pltpu.VMEM)
HBM = pl.BlockSpec(memory_space=pltpu.HBM)
SMEM = pl.BlockSpec(memory_space=pltpu.SMEM)
F32 = jnp.float32
BF16 = jnp.bfloat16


def params(mib):
    return pltpu.CompilerParams(vmem_limit_bytes=mib * 2**20)


def iota(shape, dim):
    return lax.broadcasted_iota(jnp.int32, shape, dim)


def dot_t(a, b):
    return lax.dot_general(a, b, (((1,), (1,)), ((), ())), preferred_element_type=F32)


def store_tiles(g_ref, value):
    for tile in range(g_ref.shape[0]):
        g_ref[tile] = value[:, tile * LANES : (tile + 1) * LANES]


def combine(even, odd, span):
    part = iota((1, LANES), 1) // span % 2
    swapped = pltpu.roll(odd, span, 1)
    if 2 * span < LANES:
        swapped = jnp.where(part == 0, pltpu.roll(odd, LANES - span, 1), swapped)
    return swapped + jnp.where(part == 0, 1.0, -1.0) * even


def scatter(g_ref, out_keep, out_send, seg, members, finish):
    rows = g_ref.shape[-2] // members
    for slot in range(members):
        at = pl.multiple_of((seg ^ slot) * rows, 8)
        finish(
            [g_ref[t, pl.ds(at, rows // 2, stride=2), :] for t in range(g_ref.shape[0])],
            [g_ref[t, pl.ds(at + 1, rows // 2, stride=2), :] for t in range(g_ref.shape[0])],
            out_send if slot % 2 else out_keep,
            slot // 2,
        )


def first_kernel(members, x_hbm, valid_hbm, *refs):
    row_ref, *chunk_refs, a_ref, keep_ref, send_ref, buf, valid_buf, b_ref, g_ref, sems = refs
    copies = [
        pltpu.make_async_copy(valid_hbm, valid_buf, sems.at[0]),
        pltpu.make_async_copy(x_hbm.at[:, 2:4], buf.at[:, 2:4], sems.at[1]),
        pltpu.make_async_copy(x_hbm.at[:, :2], buf.at[:, :2], sems.at[2]),
        pltpu.make_async_copy(x_hbm.at[:, 4:], buf.at[:, 4:], sems.at[3]),
    ]
    for copy in copies:
        copy.start()
    block = buf.shape[0]
    stations = block // len(chunk_refs)
    rows = 4 * stations
    half = rows // 2
    station, lane = iota((block, rows), 0), iota((block, rows), 1)
    to, frm = iota((rows, rows), 0), iota((rows, rows), 1)
    source = jnp.where(to < half, 2 * to, 2 * (to - half) + 1)
    copies[0].wait()
    valid = jnp.broadcast_to(valid_buf[...], row_ref.shape).astype(F32).astype(BF16)
    row_ref[...] = valid
    picks = []
    for k in range(len(chunk_refs)):
        spread = (lane // 4 + k * stations == station).astype(BF16)
        mask = jnp.dot(valid, spread, preferred_element_type=F32)[:1]
        picks.append(jnp.where(frm == source, jnp.broadcast_to(mask, (rows, rows)), 0.0).astype(BF16))
    pick = (iota((a_ref.shape[0], block), 0) // (a_ref.shape[0] // block) == iota((a_ref.shape[0], block), 1)).astype(BF16)
    mask = dot_t(pick, valid)[:, :1].astype(BF16)
    copies[1].wait()
    for k, chunk_ref in enumerate(chunk_refs):
        some = buf[k * stations : (k + 1) * stations, 2:4].reshape(rows, buf.shape[-1])
        chunk = jnp.dot(picks[k], some, preferred_element_type=F32).astype(BF16)
        chunk_ref[...] = chunk
        for part in range(2):
            at = part * b_ref.shape[0] // 2 + k * half
            b_ref[at : at + half] = chunk[part * half : (part + 1) * half]
    copies[2].wait()
    copies[3].wait()
    a_ref[...] = buf[...].reshape(a_ref.shape) * mask
    store_tiles(g_ref, dot_t(a_ref[...], b_ref[...]))

    def finish(even, odd, out, slot):
        out[slot, :, :LANES] = even[0] + odd[1]
        out[slot, :, LANES:] = odd[0] - even[1]

    scatter(g_ref, keep_ref, send_ref, lax.axis_index("seg"), members, finish)


def place(index):
    return (lax.axis_index("stn") >> index) & 1 == 1


def choose_kernel(own_ref, four_ref, out_ref):
    odd = place(1)

    @pl.when(odd)
    def _():
        out_ref[...] = four_ref[...]

    @pl.when(jnp.logical_not(odd))
    def _():
        out_ref[...] = own_ref[...]


def unit_kernel(members, kinds, a_ref, sib_ref, *refs):
    count = len(kinds)
    piece_refs, own_refs = refs[:count], refs[count : 2 * count]
    _, keep_ref, send_ref, b_ref, g_ref = refs[2 * count :]
    width = piece_refs[0].shape[0] // 2
    second = place(0)

    def fill(which, i, ref):
        for part in range(2):
            to = (part * count + i) * width
            b_ref[which, to : to + width] = ref[part * width : (part + 1) * width]

    for i, kind in enumerate(kinds):
        fill(0, i, piece_refs[i])
        if kind == "F":
            pl.when(second)(functools.partial(fill, 1, i, piece_refs[i]))
            pl.when(jnp.logical_not(second))(functools.partial(fill, 1, i, own_refs[i]))
        else:
            fill(1, i, piece_refs[i])
    mine, theirs = dot_t(a_ref[...], b_ref[0]), dot_t(sib_ref[...], b_ref[1])
    store_tiles(g_ref, jnp.concatenate([mine, theirs], axis=1))

    def finish(even, odd, out, slot):
        for t in range(len(even)):
            out[t, slot] = combine(even[t], odd[t], count * width)

    scatter(g_ref, keep_ref, send_ref, lax.axis_index("seg"), members, finish)


def add_kernel(keep_ref, got_ref, new_keep_ref, new_send_ref):
    for slot in range(keep_ref.shape[0]):
        out = new_send_ref if slot % 2 else new_keep_ref
        out[slot // 2] = keep_ref[slot] + got_ref[slot]


def joint_add_kernel(*refs):
    *in_refs, keep_ref, send_ref = refs
    for u in range(len(in_refs) // 2):
        for t in range(2):
            keep_ref[2 * u + t] = in_refs[2 * u][t, 0] + in_refs[2 * u + 1][t, 0]
            send_ref[2 * u + t] = in_refs[2 * u][t, 1] + in_refs[2 * u + 1][t, 1]


def home_kernel(bases, *refs):
    *in_refs, out_ref = refs
    for k, base in enumerate(bases):
        out_ref[k] = in_refs[2 * k][base + 1] + in_refs[2 * k + 1][base + 1]


def final_kernel(factor, units, bases, live_ref, *refs):
    own_keep_ref, own_got_ref, *in_refs, early_ref, late_ref, out_hbm, out_ref, sems = refs
    places = [(r, i) for r in (early_ref, late_ref) for i in range(r.shape[0])]
    width = LANES // CHUNKS
    steps = sems.shape[0]
    rows = out_ref.shape[0] // (2 * PAIRS * steps)
    copies = []
    for step in range(steps):
        some = pl.ds(step * rows, rows)
        own = own_keep_ref[some, :] + own_got_ref[some, :]
        second = jnp.broadcast_to(lax.axis_index("stn") & 1, own[:, :LANES].shape) == 1
        columns = {}
        for u, unit in enumerate(units):
            mine = in_refs[2 * u][bases[u], some, :] + in_refs[2 * u + 1][bases[u], some, :]
            theirs = places[u][0][places[u][1], some, :]
            for i, (kind, k) in enumerate(unit):
                for part in range(2):
                    at = (part * len(unit) + i) * width
                    columns[kind, k, part] = mine[:, at : at + width]
                    columns[kind + "s", k, part] = theirs[:, at : at + width]
        for part in range(2):
            four, two, mine_two, mine_four = (
                jnp.concatenate([columns[kind, k, part] for k in range(CHUNKS)], axis=1)
                for kind in ("Fs", "Xs", "X", "F")
            )
            values = [
                own[:, part * LANES : (part + 1) * LANES],
                jnp.where(second, four, two),
                mine_two,
                jnp.where(second, two, four),
                mine_four,
            ]
            for offset, value in enumerate(values):
                scale = live_ref[0, offset].astype(F32) * factor
                to = step * rows * 2 * PAIRS + 2 * offset + part
                out_ref[pl.ds(to, rows, stride=2 * PAIRS), :] = value * scale
        slab = pl.ds(step * rows * 2 * PAIRS, rows * 2 * PAIRS)
        copies.append(pltpu.make_async_copy(out_ref.at[slab], out_hbm.at[slab], sems.at[step]))
        copies[-1].start()
    for copy in copies:
        copy.wait()


def tie(values, *others):
    return lax.optimization_barrier((values, others))[0] if others else values


def per_device(spectra, segment_valid, pair_live):
    block, channels, seg_local, _, freq = spectra.shape
    blocks, members = lax.axis_size("stn"), lax.axis_size("seg")
    factor = 1.0 / math.sqrt(seg_local * members * freq)
    rows, per, half = 2 * block * channels, block * channels // members, members // 2
    width = 2 * block // CHUNKS
    ids = range(blocks)

    def call(kernel, outs, operands, mib, scratch=(), specs=None, out_spec=VMEM):
        return pl.pallas_call(
            kernel,
            in_specs=specs or [VMEM] * len(operands),
            out_specs=[out_spec] * len(outs),
            out_shape=[jax.ShapeDtypeStruct(*out) for out in outs],
            scratch_shapes=list(scratch),
            compiler_params=params(mib),
        )(*operands)

    valid, *own, a, keep, send = call(
        functools.partial(first_kernel, members),
        [((8, block), BF16)]
        + [((2 * width, freq), BF16)] * CHUNKS
        + [((rows, freq), BF16)]
        + [((half, per, 4 * block), F32)] * 2,
        [pltpu.with_memory_space_constraint(v, pltpu.HBM) for v in (spectra, segment_valid.reshape(1, block))],
        16,
        [
            pltpu.VMEM((block, channels, 1, 2, freq), BF16),
            pltpu.VMEM((1, block), jnp.int32),
            pltpu.VMEM((4 * block, freq), BF16),
            pltpu.VMEM((4 * block // LANES, rows, LANES), F32),
            pltpu.SemaphoreType.DMA((4,)),
        ],
        [HBM] * 2,
    )

    def exchange(c, distance):
        return lax.ppermute(c, "stn", [(i ^ distance, i) for i in ids])

    def halve(keep, send, distance, kinds):
        got = lax.ppermute(send, "seg", [(i ^ distance, i) for i in range(members)])
        lead = (kinds,) if kinds else ()
        slots = keep.shape[len(lead)]
        if slots == 1:
            return keep.reshape(*lead, *keep.shape[-2:]), got.reshape(*lead, *keep.shape[-2:])
        shape = (max(kinds, 1) * slots // 2, *keep.shape[-2:])
        new = call(add_kernel, [(shape, F32)] * 2, [v.reshape(-1, *shape[1:]) for v in (keep, got)], 8)
        return [v.reshape(*lead, slots // 2, *shape[1:]) for v in new]

    def reduce(keep, send, kinds, name):
        distance = 1
        while distance < members:
            if 2 * distance == members:
                send = tie(send, *after(name + "b"))
            keep, send = halve(keep, send, distance, kinds)
            done[name + ("a" if distance == 1 else "b")] = keep if 2 * distance < members else send
            distance *= 2
        return keep, send

    done = {}

    def after(name):
        return [done[n] for n in TIES.get(name, ())]

    sibling = exchange(tie(a, *after("S")), 1)
    done["S"] = sibling

    def four_of(k):
        value = tie(own[k], *after("F%d" % k))
        done["F%d" % k] = lax.ppermute(value, "stn", [((i - 4) % blocks, i) for i in ids])
        return done["F%d" % k]

    def two_of(k):
        value = tie(own[k], *after("X%d" % k))
        (c,) = call(choose_kernel, [((2 * width, freq), BF16)], [value, four[k]], 8)
        done["X%d" % k] = exchange(c, 2)
        return done["X%d" % k]

    def unit(name):
        pieces = [(name[i], int(name[i + 1])) for i in range(0, len(name), 2)]
        columns = 2 * width * len(pieces)
        tiles = max(1, 2 * columns // LANES)
        keep, send = call(
            functools.partial(unit_kernel, members, [p[0] for p in pieces]),
            [((tiles, half, per, LANES), F32)] * 2,
            [a, sibling]
            + [(four if kind == "F" else two)[k] for kind, k in pieces]
            + [own[k] for _, k in pieces]
            + [tie(valid, *after(name))],
            16,
            [pltpu.VMEM((2, columns, freq), BF16), pltpu.VMEM((tiles, rows, LANES), F32)],
        )
        done[name + "k"] = keep
        if name not in JOINT:
            return pieces, reduce(keep, send, tiles, name), 0
        distance = 1
        while 4 * distance < members:
            keep, send = halve(keep, send, distance, tiles)
            distance *= 2
        got = lax.ppermute(send, "seg", [(i ^ distance, i) for i in range(members)])
        done[name + "a"] = got
        held.extend([keep, got])
        if len(held) == 2 * len(JOINT):
            shape = (2 * len(JOINT), per, LANES)
            kept, sent = call(joint_add_kernel, [(shape, F32)] * 2, held, 8)
            distance = members // 2
            done["J"] = lax.ppermute(sent, "seg", [(i ^ distance, i) for i in range(members)])
            joint.extend([kept, done["J"]])
        return pieces, joint, 2 * (len(held) // 2 - 1)

    four, two, held, joint = [], [], [], []
    units = []
    for name in ORDER:
        if name == "U":
            own_keep, own_got = reduce(keep, send, 0, "U")
        elif len(name) == 2 and name[0] == "F" and len(four) <= int(name[1]):
            four.append(four_of(int(name[1])))
        elif len(name) == 2 and name[0] == "X" and len(two) <= int(name[1]):
            two.append(two_of(int(name[1])))
        else:
            units.append(unit(name))
    bases = [base for _, _, base in units]
    pieces = [piece for _, piece, _ in units]
    units = [names for names, _, _ in units]
    early = [v for piece in pieces[:-1] for v in piece]
    (early_home,) = call(functools.partial(home_kernel, bases[:-1]), [((len(pieces) - 1, per, LANES), F32)], early, 8)
    (late_home,) = call(functools.partial(home_kernel, bases[-1:]), [((1, per, LANES), F32)], pieces[-1], 8)
    sums = [v for piece in pieces for v in piece]
    operands = [pair_live, own_keep, own_got, *sums, exchange(early_home, 1), exchange(late_home, 1)]
    (out,) = call(
        functools.partial(final_kernel, factor, units, bases),
        [((2 * PAIRS * per, 2 * block), F32)],
        operands,
        12,
        [
            pltpu.VMEM((2 * PAIRS * per, 2 * block), F32),
            pltpu.SemaphoreType.DMA((STEPS if per % (8 * STEPS) == 0 else 1,)),
        ],
        [SMEM] + [VMEM] * (len(operands) - 1),
        HBM,
    )
    return out.reshape(block // members, channels, PAIRS, 2, 2 * block)


def solution(mesh):
    return jax.shard_map(
        per_device,
        mesh=mesh,
        in_specs=(P("stn", None, "seg", None, None), P("stn", "seg"), P("stn", None)),
        out_specs=P(("stn", "seg"), None, None, None, None),
        check_vma=False,
    )
```
